256 devices in a mesh: leaf: 32 (over z, x), rhs: 8 (over y, core).
Axes of the slice: x: 4, y: 4, z: 8, core: 2. Of those that a mesh axis runs over, the one named last changes fastest.
Arguments:
- charges: float32 [24576, 8192], P('leaf', 'rhs'), parts along dimension 1, may hold values from -6 to 6
- near_blocks: float32 [32, 3, 768, 768], P('leaf'), may hold values from -0.125 to 0.125
- neighbours: int32 [32, 2], P('leaf'), may hold values from 0 to 31, as said below
- compress: float32 [32, 768, 192], P('leaf'), may hold values from -0.21875 to 0.21875
- transfer: float32 [32, 5, 2, 192, 192], P('leaf'), may hold values from -0.3125 to 0.3125
- expand: float32 [32, 768, 192], P('leaf'), may hold values from -0.4375 to 0.4375
Outputs:
- potential: float32 [24576, 8192], P('leaf', 'rhs'), parts along dimension 1
The draws below stay inside these ranges and needn't reach their ends.
There are 8 independent parts, one for each index of `rhs`. The reference program is written for one: setup_inputs(seed, part) draws one part's arguments, and reference() takes and returns one part's arrays. A program takes and returns all parts, laid end to end along the dimension named above; an argument that names none is the same for every part. Nothing has to cross between parts.
Inputs may be any that keep to these rules, and one draw needn't show every extreme that they name: `neighbours`: row i lists two different leaves, each of (i - 2), (i - 1), (i + 1), (i + 2) modulo 32; never i itself.
All inputs are finite; a program needn't handle non-finite values.
Results may differ from the reference program's by a relative error of at most 0.0001.
Values sent between devices are 32-bit elements; how exact they have to be, the bound alone decides.
A program may use at most 128 MiB of HBM per device.

```python
import jax
import jax.numpy as jnp
from jax import lax

LEAF_ROWS = 768
RANK = 192
COLS = 1024
LEAVES = 32
LEVELS = 5
ROWS = 24576


def draw_neighbours(key, part):
    key_one = jax.random.fold_in(key, 11)
    key_two = jax.random.fold_in(key, 23)
    first = jax.random.randint(key_one, (LEAVES,), 0, 4)
    second = (first + jax.random.randint(key_two, (LEAVES,), 1, 4)) % 4
    picks = jnp.stack([first, second], axis=1)
    offsets = jnp.where(picks < 2, picks - 2, picks - 1)
    leaf_ids = jnp.arange(LEAVES, dtype=jnp.int32)[:, None]
    return ((leaf_ids + offsets) % LEAVES).astype(jnp.int32)


def block_levels(key, extent, split, smallest, largest):
    def one(axis_at, shards_of):
        draws = jax.random.uniform(jax.random.fold_in(jax.random.fold_in(key, 6), axis_at), (shards_of,), jnp.float32, smallest / len(split), largest / len(split))
        return jnp.repeat(jnp.exp(draws), extent[axis_at] // shards_of).reshape((-1,) + (1,) * (len(extent) - axis_at - 1))

    loudness = one(*split[0])
    for cut in split[1:]:
        loudness = loudness * one(*cut)
    return loudness


def bell_draw(stream_key, extent, spread, bound, shards=(), kind=jnp.bfloat16):
    array = jax.random.normal(stream_key, extent, jnp.float32) * spread
    if len(shards) > 0:
        array = block_levels(stream_key, extent, shards, -0.22, 0.18) * array
    return jnp.clip(array, min=-bound, max=bound).astype(kind)


def setup_inputs(seed: int = 0, part: int = 0) -> dict:
    seeds = jax.random.split(jax.random.key(seed), 7)
    part_keys = jax.random.split(jax.random.fold_in(seeds[6], part), 7)
    return {
        "charges": bell_draw(part_keys[0], (ROWS, COLS), 1.0, 6.0, ((0, 32),), jnp.float32),
        "near_blocks": bell_draw(seeds[1], (LEAVES, 3, LEAF_ROWS, LEAF_ROWS), (3 * LEAF_ROWS) ** -0.5, 0.125, ((0, 32),), jnp.float32),
        "neighbours": draw_neighbours(jax.random.fold_in(seeds[6], 71), part),
        "compress": bell_draw(seeds[3], (LEAVES, LEAF_ROWS, RANK), LEAF_ROWS ** -0.5, 0.21875, ((0, 32),), jnp.float32),
        "transfer": bell_draw(seeds[4], (LEAVES, LEVELS, 2, RANK, RANK), (2 * RANK) ** -0.5, 0.3125, ((0, 32),), jnp.float32),
        "expand": bell_draw(seeds[5], (LEAVES, LEAF_ROWS, RANK), RANK ** -0.5, 0.4375, ((0, 32),), jnp.float32),
    }


def reference(charges, near_blocks, neighbours, compress, transfer, expand):
    hi = lax.Precision.HIGHEST
    blocks = charges.reshape(LEAVES, LEAF_ROWS, COLS)
    first = blocks[neighbours[:, 0]]
    second = blocks[neighbours[:, 1]]
    near = jnp.einsum('lab,lbc->lac', near_blocks[:, 0], blocks, precision=hi)
    near = near + jnp.einsum('lab,lbc->lac', near_blocks[:, 1], first, precision=hi)
    near = near + jnp.einsum('lab,lbc->lac', near_blocks[:, 2], second, precision=hi)
    coeffs = jnp.einsum('lar,lac->lrc', compress, blocks, precision=hi)
    leaf_ids = jnp.arange(LEAVES, dtype=jnp.int32)
    for level in range(LEVELS):
        partner_ids = jnp.bitwise_xor(leaf_ids, jnp.int32(1 << level))
        partner_coeffs = coeffs[partner_ids]
        coeffs = jnp.einsum('lrs,lsc->lrc', transfer[:, level, 0], coeffs, precision=hi) + jnp.einsum('lrs,lsc->lrc', transfer[:, level, 1], partner_coeffs, precision=hi)
    far = jnp.einsum('lar,lrc->lac', expand, coeffs, precision=hi)
    return (near + far).reshape(LEAVES * LEAF_ROWS, COLS)
```

```python
import functools

import jax
import jax.numpy as jnp
from jax import lax
from jax.experimental import pallas as pl
from jax.experimental.pallas import tpu as pltpu
from jax.sharding import PartitionSpec as P

F32, BF16 = jnp.float32, jnp.bfloat16
XS = 4
PARTS = 4
ROUNDS = 6
COUNT = {"P": 2, "Q": 4}
SLOTS = (("A1", "P", 4), ("A1", "Q", 2), ("A2", "P", 2), ("A2", "Q", 4), ("A3", "P", 4),
         ("A3", "Q", 2), ("ZR", "P", 2), ("ZR", "Q", 4), ("Z0", "Q", 4))
BASE, HOLD = {}, 0
for _slot, _link, _count in SLOTS:
    BASE[_slot, _link] = HOLD
    HOLD += _count
OTHER = {"P": "Q", "Q": "P"}
PLUS = {-2: 0, -1: 1, 1: 2, 2: 3}
OWN = 4
RELAYED = (0, 2)

ORDER = (
    "own Q 0", "comp 0", "prep 4", "comp 1", "prep 0", "L 0 0", "L 0 1", "own Q 1", "Z0 0",
    "prep 2", "comp 3", "comp 2", "L 1 1", "ownmm 0", "L 0 3", "prep 1", "own P 0", "Z0 1",
    "L 2 1", "L 0 2", "L 1 0", "own Q 2", "L 2 0", "ownmm 1", "prep 3", "L 1 3", "A1 Q 0", "L 3 1",
    "A1 P 0", "L 2 3", "L 1 2", "own P 1", "Z0 2", "A2 P 0", "A1 P 1", "own Q 3", "L 2 2",
    "A1 P 2", "A2 Q 0", "Z0 3", "L 3 0", "A1 Q 1", "ZR Q 0", "A2 Q 1", "L 3 2", "ZR P 0", "A2 Q 2",
    "A1 P 3", "A3 Q 0", "ZR Q 1", "A2 P 1", "R 0", "R 2", "A3 P 0", "A2 Q 3", "ZR Q 2", "A3 P 1",
    "L 3 3", "ZR P 1", "ZR Q 3", "L 4 2", "A3 P 2", "L 4 1", "L 4 0", "A3 P 3", "A3 Q 1", "L 4 3",
)


def tokens():
    for token in ORDER:
        name, *args = token.split()
        yield name, args


def split(value):
    high = value.astype(BF16)
    return high, (value - high.astype(F32)).astype(BF16)


def three(value):
    high, low = split(value)
    return jnp.concatenate([high, low, high], axis=0)


def matmul(left, right):
    return jnp.dot(left, right, preferred_element_type=F32)


def kernel(zs, nb, x_hbm, near_hbm, compress_hbm, transfer_hbm, expand_hbm, out,
           xv, x_high, x_low, got, w_high, w_low, near, comp, comp3, trans, trans6,
           expa, expa3, sent, came, mid, load_sem, near_send, near_recv, far_send, far_recv,
           mid_send, mid_recv):
    rows, cols = out.shape
    tall, wide = rows // ROUNDS, cols // PARTS
    rank = comp3.shape[0]
    leaf, r = lax.axis_index("leaf"), lax.axis_index("rhs")
    x, z = leaf % XS, leaf // XS
    odd = x % 2
    step = {"P": 1 - 2 * odd, "Q": 2 * odd - 1}
    end = jnp.logical_or(x == 0, x == XS - 1)
    middle = jnp.logical_not(end)

    def chip(dx, dz):
        return ((z + dz + zs) % zs) * XS + (x + dx + XS) % XS, r

    def partner(level):
        bit = (leaf // 2**level) % 2
        return leaf + (1 - 2 * bit) * 2**level, r

    def load(i, src, dst):
        return pltpu.make_async_copy(src, dst, load_sem.at[i])

    loads = {
        "comp": load(0, compress_hbm, comp),
        "x": load(1, x_hbm, xv),
        "trans": load(2, transfer_hbm, trans),
        "near": load(3, near_hbm, near),
        "expa": load(4, expand_hbm, expa),
    }
    for item in loads.values():
        item.start()

    barrier = pltpu.get_barrier_semaphore()
    greeted = [chip(1, 0), chip(-1, 0), partner(1), chip(0, 1), chip(0, -1), chip(0, 2),
               chip(0, -2), partner(4)]
    for device in greeted:
        pl.semaphore_signal(barrier, inc=1, device_id=device, device_id_type=pl.DeviceIdType.MESH)
    pl.semaphore_wait(barrier, len(greeted))

    def remote(src, dst, send, recv, device):
        return pltpu.make_async_remote_copy(
            src_ref=src, dst_ref=dst, send_sem=send, recv_sem=recv,
            device_id=device, device_id_type=pl.DeviceIdType.MESH)

    def near_copy(send, src, slot, link, m, device):
        at = BASE[slot, link] + m
        return remote(src, got.at[at], near_send.at[send], near_recv.at[at], device)

    def own_rows(link, m):
        first = jnp.where(step[link] == 1, 0, ROUNDS - COUNT[link])
        return x_hbm.at[pl.ds(pl.multiple_of(tall * (first + m), tall), tall)]

    def own_copy(link, m):
        return near_copy(HOLD + m + 4 * (link == "P"), own_rows(link, m), "A1", OTHER[link], m,
                         chip(step[link], 0))

    def lift_copy(m):
        return near_copy(HOLD + m, own_rows("Q", m), "Z0", "Q", m, chip(0, step["Q"]))

    def pass_copy(slot, link, m):
        source = BASE[slot, link] + m
        to = {"Z0": "A1", "A1": "A2", "A2": "A3", "ZR": "A3"}[slot]
        send = BASE["A3", OTHER[link]] + m if to == "A3" else source
        return near_copy(send, got.at[source], to, OTHER[link], m, chip(step[link], 0))

    def z_copy(link, m):
        h = jnp.where(step[link] == 1, 0, 1)
        wraps = x == (XS - 1) * h
        dz = jnp.where(wraps, 1, -1) * step[link]
        source = BASE["A2", link] + m
        return near_copy(source, got.at[source], "ZR", link, m, chip(0, dz))

    def arrived(slot, link, m):
        at = BASE[slot, link] + m
        remote(got.at[at], got.at[at], near_send.at[at], near_recv.at[at], chip(1, 0)).wait_recv()

    def weight_of(slot, link):
        h = jnp.where(step[link] == 1, 0, 1)
        if slot == "A1":
            return 1 + h
        if slot == "A3":
            return 2 - h
        wraps = x == (XS - 1) * h
        ahead, behind = 3 - 3 * h, 3 * h
        if slot == "A2":
            return jnp.where(wraps, ahead, behind)
        return jnp.where(wraps, behind, ahead)

    def near_product(slot, link, m):
        which = weight_of(slot, link)
        count = dict(((a, b), c) for a, b, c in SLOTS)[slot, link]
        first = jnp.where(step[link] == 1, 0, ROUNDS - count) + m
        at = BASE[slot, link] + m
        high = [w_high[which, first + i] for i in range(2)]
        low = [w_low[which, first + i] for i in range(2)]
        left = jnp.concatenate(high + high + low, axis=1)
        for to in (slice(0, cols // 2), slice(cols // 2, cols)):
            value = jnp.concatenate([got[at, :, to], got[at + 1, :, to]], axis=0)
            out[:, to] = out[:, to] + matmul(left, three(value))

    def far_copy(level, k):
        return remote(sent.at[level, k], came.at[level, k], far_send.at[level, k],
                      far_recv.at[level, k], partner(level))

    two_on = chip(0, 4 * odd - 2)

    def first_leg(k):
        i = RELAYED.index(k)
        return remote(sent.at[4, k], mid.at[i], far_send.at[4, k], mid_recv.at[i], two_on)

    def second_leg(k):
        i = RELAYED.index(k)
        return remote(mid.at[i], came.at[4, k], mid_send.at[i], far_recv.at[4, k], two_on)

    here = [pl.ds(wide * k, wide) for k in range(PARTS)]
    waited = set()

    def need(name):
        if name not in waited:
            waited.add(name)
            loads[name].wait()

    def prepare(which):
        need("near")
        if which == OWN:
            scales = None
        else:
            offset = {v: k for k, v in PLUS.items()}[which]
            count = zs * XS
            scales = [
                jnp.where((nb[0, j] - leaf - offset + 2 * count) % count == 0, 1.0, 0.0).astype(F32)
                for j in range(2)
            ]

        def body(i, carry):
            at = pl.ds(pl.multiple_of(i * tall, tall), tall)
            if scales is None:
                value = near[0, at, :]
            else:
                value = scales[0] * near[1, at, :] + scales[1] * near[2, at, :]
            high, low = split(value)
            for c in range(ROUNDS):
                w_high[which, c, at, :] = high[:, tall * c:tall * (c + 1)]
                w_low[which, c, at, :] = low[:, tall * c:tall * (c + 1)]
            return carry

        lax.fori_loop(0, ROUNDS, body, 0)

    for name, args in tokens():
        if name == "own":
            link, m = args[0], int(args[1])
            if link == "P":
                own_copy(link, m).start()
            else:
                @pl.when(end)
                def _():
                    lift_copy(m).start()

                @pl.when(middle)
                def _():
                    own_copy(link, m).start()
        elif name == "comp":
            k = int(args[0])
            if "comp" not in waited:
                need("comp")
                high, low = split(comp[...].T)
                comp3[:, :rows] = high
                comp3[:, rows:2 * rows] = high
                comp3[:, 2 * rows:] = low
                need("x")
            high, low = split(xv[:, here[k]])
            x_high[:, here[k]] = high
            x_low[:, here[k]] = low
            sent[0, k] = matmul(comp3[...], jnp.concatenate([high, low, high], axis=0))
            far_copy(0, k).start()
        elif name == "L":
            level, k = int(args[0]), int(args[1])
            if "trans" not in waited:
                need("trans")
                for i in range(5):
                    for j in range(2):
                        high, low = split(trans[2 * i + j])
                        at = 3 * rank * j
                        trans6[i, :, at:at + rank] = high
                        trans6[i, :, at + rank:at + 2 * rank] = high
                        trans6[i, :, at + 2 * rank:at + 3 * rank] = low
            far_copy(level, k).wait_recv()
            both = jnp.concatenate([three(sent[level, k]), three(came[level, k])], axis=0)
            coeffs = matmul(trans6[level], both)
            if level < 4:
                sent[level + 1, k] = coeffs
                if level == 3 and k in RELAYED:
                    first_leg(k).start()
                else:
                    far_copy(level + 1, k).start()
            else:
                if "expa" not in waited:
                    need("expa")
                    high, low = split(expa[...])
                    expa3[:, :rank] = high
                    expa3[:, rank:2 * rank] = high
                    expa3[:, 2 * rank:] = low
                out[:, here[k]] = out[:, here[k]] + matmul(expa3[...], three(coeffs))
        elif name == "R":
            k = int(args[0])
            first_leg(k).wait_recv()
            second_leg(k).start()
        elif name == "prep":
            prepare(int(args[0]))
        elif name == "ownmm":
            at = slice(cols // 2 * int(args[0]), cols // 2 * (int(args[0]) + 1))
            high = [w_high[OWN, c] for c in range(ROUNDS)]
            low = [w_low[OWN, c] for c in range(ROUNDS)]
            left = jnp.concatenate(high + high + low, axis=1)
            right = jnp.concatenate([x_high[:, at], x_low[:, at], x_high[:, at]], axis=0)
            out[:, at] = matmul(left, right)
        elif name == "Z0":
            m = int(args[0])

            @pl.when(end)
            def _():
                arrived("Z0", "Q", m)
                pass_copy("Z0", "Q", m).start()
        else:
            link, m = args[0], int(args[1])
            arrived(name, link, m)
            if name == "A1":
                pass_copy("A1", link, m).start()
            if name == "A2":
                z_copy(link, m).start()

                @pl.when(end)
                def _():
                    pass_copy("A2", link, m).start()
            if name == "ZR":
                @pl.when(middle)
                def _():
                    pass_copy("ZR", link, m).start()
            if m % 2:
                near_product(name, link, m - 1)

    for link in "PQ":
        for m in range(COUNT[link]):
            own_copy(link, m).wait_send()
            z_copy(link, m).wait_send()
            pass_copy("A2", link, m).wait_send()
        for m in range(COUNT[OTHER[link]]):
            pass_copy("A1", link, m).wait_send()

    @pl.when(end)
    def _():
        for m in range(COUNT["Q"]):
            pass_copy("Z0", "Q", m).wait_send()

    for level in range(5):
        for k in range(PARTS):
            far_copy(level, k).wait_send()
    for k in RELAYED:
        second_leg(k).wait_send()


def per_device(charges, near_blocks, neighbours, compress, transfer, expand):
    rows, cols = charges.shape
    rank = compress.shape[2]
    leaves = lax.axis_size("leaf")
    tall, wide = rows // ROUNDS, cols // PARTS
    anywhere = pl.BlockSpec(memory_space=pl.ANY)
    dma = pltpu.SemaphoreType.DMA
    vmem = pltpu.VMEM
    return pl.pallas_call(
        functools.partial(kernel, leaves // XS),
        out_shape=jax.ShapeDtypeStruct((rows, cols), F32),
        in_specs=[pl.BlockSpec(memory_space=pltpu.SMEM)] + [anywhere] * 5,
        out_specs=pl.BlockSpec(memory_space=pltpu.VMEM),
        scratch_shapes=[
            vmem((rows, cols), F32),
            vmem((rows, cols), BF16),
            vmem((rows, cols), BF16),
            vmem((HOLD, tall, cols), F32),
            vmem((5, ROUNDS, rows, tall), BF16),
            vmem((5, ROUNDS, rows, tall), BF16),
            vmem((3, rows, rows), F32),
            vmem((rows, rank), F32),
            vmem((rank, 3 * rows), BF16),
            vmem((10, rank, rank), F32),
            vmem((5, rank, 6 * rank), BF16),
            vmem((rows, rank), F32),
            vmem((rows, 3 * rank), BF16),
            vmem((5, PARTS, rank, wide), F32),
            vmem((5, PARTS, rank, wide), F32),
            vmem((len(RELAYED), rank, wide), F32),
            dma((5,)),
            dma((HOLD + ROUNDS,)),
            dma((HOLD,)),
            dma((5, PARTS)),
            dma((5, PARTS)),
            dma((len(RELAYED),)),
            dma((len(RELAYED),)),
        ],
        compiler_params=pltpu.CompilerParams(
            collective_id=0, has_side_effects=True, vmem_limit_bytes=63 << 20),
        name="operator",
    )(
        neighbours,
        charges,
        near_blocks[0],
        compress[0],
        transfer[0].reshape(10, rank, rank),
        expand[0],
    )


def solution(mesh):
    in_specs = (
        P("leaf", "rhs"),
        P("leaf", None, None, None),
        P("leaf", None),
        P("leaf", None, None),
        P("leaf", None, None, None, None),
        P("leaf", None, None),
    )
    out_specs = P("leaf", "rhs")
    return jax.shard_map(
        per_device, mesh=mesh, in_specs=in_specs, out_specs=out_specs, check_vma=False
    )
```

```python
import functools

import jax
import jax.numpy as jnp
from jax import lax
from jax.experimental import pallas as pl
from jax.experimental.pallas import tpu as pltpu
from jax.sharding import PartitionSpec as P

F32, BF16 = jnp.float32, jnp.bfloat16
XS = 4
PARTS = 4
ROUNDS = 12
TOGETHER = 4
LANES = 128
COUNT = {"P": 4, "Q": 8}
SLOTS = (("A1", "P", 8), ("A1", "Q", 4), ("A2", "P", 4), ("A2", "Q", 8), ("A3", "P", 8),
         ("A3", "Q", 4), ("ZR", "P", 4), ("ZR", "Q", 8), ("Z0", "Q", 8))
BASE, HOLD = {}, 0
for _slot, _link, _count in SLOTS:
    BASE[_slot, _link] = HOLD
    HOLD += _count
OTHER = {"P": "Q", "Q": "P"}
PLUS = {-2: 0, -1: 1, 1: 2, 2: 3}
OWN = 4
RELAYED = (0, 2, 3)

ORDER = (
    "own Q 0", "own Q 1", "comp 0", "prep 4", "comp 1", "L 0 0", "prep 2", "L 0 1", "own Q 2",
    "comp 3", "Z0 0", "comp 2", "prep 3", "L 1 0", "Z0 1", "own Q 3", "ownmm 1", "L 2 0",
    "own P 0", "prep 1", "L 1 1", "ownmm 0", "own Q 4", "Z0 2", "prep 0", "own P 1", "A1 Q 0",
    "L 2 1", "A1 P 0", "L 0 3", "Z0 3", "L 3 0", "A2 P 0", "L 0 2", "A1 Q 1", "own P 2", "A1 P 1",
    "L 3 1", "Z0 4", "own P 3", "L 1 3", "own Q 5", "A2 Q 0", "L 2 3", "A1 P 2", "A1 P 3",
    "own Q 6", "A2 P 1", "ZR P 0", "A1 Q 2", "A2 Q 1", "L 1 2", "R 0", "Z0 5", "own Q 7", "ZR Q 0",
    "A2 P 2", "A1 Q 3", "ZR P 1", "L 4 1", "A2 Q 2", "Z0 6", "A1 P 4", "A2 Q 3", "L 2 2", "A1 P 5",
    "Z0 7", "L 3 3", "ZR Q 1", "A2 Q 4", "ZR Q 2", "A1 P 6", "ZR Q 3", "A3 P 0", "A2 Q 5", "L 3 2",
    "ZR P 2", "ZR Q 4", "L 4 0", "A3 Q 0", "A2 Q 6", "A3 P 1", "ZR Q 5", "A1 P 7", "A3 Q 1",
    "A2 P 3", "R 3", "ZR Q 6", "A3 P 2", "A3 Q 2", "A3 P 3", "A3 P 4", "A2 Q 7", "R 2", "A3 P 5",
    "ZR P 3", "A3 Q 3", "ZR Q 7", "L 4 3", "A3 P 6", "A3 P 7", "L 4 2",
)


def tokens():
    for token in ORDER:
        name, *args = token.split()
        yield name, args


def split(value):
    high = value.astype(BF16)
    return high, (value - high.astype(F32)).astype(BF16)


def three(value):
    high, low = split(value)
    return jnp.concatenate([high, low, high], axis=0)


def matmul(left, right):
    return jnp.dot(left, right, preferred_element_type=F32)


def kernel(zs, nb, x_hbm, near_hbm, compress_hbm, transfer_hbm, expand_hbm, out,
           xv, x_high, x_low, got, w_high, w_low, near, comp, comp3, trans, trans6,
           expa, expa3, sent, came, mid, load_sem, near_send, near_recv, far_send, far_recv,
           mid_send, mid_recv):
    rows, cols = out.shape
    tall, wide = rows // ROUNDS, cols // PARTS
    rank = comp3.shape[0]
    leaf, r = lax.axis_index("leaf"), lax.axis_index("rhs")
    x, z = leaf % XS, leaf // XS
    odd = x % 2
    step = {"P": 1 - 2 * odd, "Q": 2 * odd - 1}
    end = jnp.logical_or(x == 0, x == XS - 1)
    middle = jnp.logical_not(end)

    def chip(dx, dz):
        return ((z + dz + zs) % zs) * XS + (x + dx + XS) % XS, r

    def partner(level):
        bit = (leaf // 2**level) % 2
        return leaf + (1 - 2 * bit) * 2**level, r

    def load(i, src, dst):
        return pltpu.make_async_copy(src, dst, load_sem.at[i])

    loads = {
        "comp": load(0, compress_hbm, comp),
        "x": load(1, x_hbm, xv),
        "trans": load(2, transfer_hbm, trans),
        "near": load(3, near_hbm, near),
        "expa": load(4, expand_hbm, expa),
    }
    for item in loads.values():
        item.start()

    barrier = pltpu.get_barrier_semaphore()
    greeted = [chip(1, 0), chip(-1, 0), partner(1), chip(0, 1), chip(0, -1), chip(0, 2),
               chip(0, -2), partner(4)]
    for device in greeted:
        pl.semaphore_signal(barrier, inc=1, device_id=device, device_id_type=pl.DeviceIdType.MESH)
    pl.semaphore_wait(barrier, len(greeted))

    def remote(src, dst, send, recv, device):
        return pltpu.make_async_remote_copy(
            src_ref=src, dst_ref=dst, send_sem=send, recv_sem=recv,
            device_id=device, device_id_type=pl.DeviceIdType.MESH)

    def near_copy(send, src, slot, link, m, device):
        at = BASE[slot, link] + m
        return remote(src, got.at[at], near_send.at[send], near_recv.at[at], device)

    def own_rows(link, m):
        first = jnp.where(step[link] == 1, 0, ROUNDS - COUNT[link])
        return x_hbm.at[pl.ds(pl.multiple_of(tall * (first + m), tall), tall)]

    def own_copy(link, m):
        return near_copy(HOLD + m + COUNT["Q"] * (link == "P"), own_rows(link, m), "A1", OTHER[link], m,
                         chip(step[link], 0))

    def lift_copy(m):
        return near_copy(HOLD + m, own_rows("Q", m), "Z0", "Q", m, chip(0, step["Q"]))

    def pass_copy(slot, link, m):
        source = BASE[slot, link] + m
        to = {"Z0": "A1", "A1": "A2", "A2": "A3", "ZR": "A3"}[slot]
        send = BASE["A3", OTHER[link]] + m if to == "A3" else source
        return near_copy(send, got.at[source], to, OTHER[link], m, chip(step[link], 0))

    def z_copy(link, m):
        h = jnp.where(step[link] == 1, 0, 1)
        wraps = x == (XS - 1) * h
        dz = jnp.where(wraps, 1, -1) * step[link]
        source = BASE["A2", link] + m
        return near_copy(source, got.at[source], "ZR", link, m, chip(0, dz))

    def arrived(slot, link, m):
        at = BASE[slot, link] + m
        remote(got.at[at], got.at[at], near_send.at[at], near_recv.at[at], chip(1, 0)).wait_recv()

    def weight_of(slot, link):
        h = jnp.where(step[link] == 1, 0, 1)
        if slot == "A1":
            return 1 + h
        if slot == "A3":
            return 2 - h
        wraps = x == (XS - 1) * h
        ahead, behind = 3 - 3 * h, 3 * h
        if slot == "A2":
            return jnp.where(wraps, ahead, behind)
        return jnp.where(wraps, behind, ahead)

    def near_product(slot, link, m):
        which = weight_of(slot, link)
        count = dict(((a, b), c) for a, b, c in SLOTS)[slot, link]
        first = (jnp.where(step[link] == 1, 0, ROUNDS - count) + m) * tall // LANES
        at = BASE[slot, link] + m
        pieces = TOGETHER * tall // LANES
        high = [w_high[which, first + i] for i in range(pieces)]
        low = [w_low[which, first + i] for i in range(pieces)]
        left = jnp.concatenate(high + high + low, axis=1)
        for to in (slice(0, cols // 2), slice(cols // 2, cols)):
            value = jnp.concatenate([got[at + i, :, to] for i in range(TOGETHER)], axis=0)
            out[:, to] = out[:, to] + matmul(left, three(value))

    def far_copy(level, k):
        return remote(sent.at[level, k], came.at[level, k], far_send.at[level, k],
                      far_recv.at[level, k], partner(level))

    two_on = chip(0, 4 * odd - 2)

    def first_leg(k):
        i = RELAYED.index(k)
        return remote(sent.at[4, k], mid.at[i], far_send.at[4, k], mid_recv.at[i], two_on)

    def second_leg(k):
        i = RELAYED.index(k)
        return remote(mid.at[i], came.at[4, k], mid_send.at[i], far_recv.at[4, k], two_on)

    here = [pl.ds(wide * k, wide) for k in range(PARTS)]
    waited = set()

    def need(name):
        if name not in waited:
            waited.add(name)
            loads[name].wait()

    def prepare(which):
        need("near")
        if which == OWN:
            scales = None
        else:
            offset = {v: k for k, v in PLUS.items()}[which]
            count = zs * XS
            scales = [
                jnp.where((nb[0, j] - leaf - offset + 2 * count) % count == 0, 1.0, 0.0).astype(F32)
                for j in range(2)
            ]

        def body(i, carry):
            at = pl.ds(pl.multiple_of(i * LANES, LANES), LANES)
            if scales is None:
                value = near[0, at, :]
            else:
                value = scales[0] * near[1, at, :] + scales[1] * near[2, at, :]
            high, low = split(value)
            for c in range(rows // LANES):
                w_high[which, c, at, :] = high[:, LANES * c:LANES * (c + 1)]
                w_low[which, c, at, :] = low[:, LANES * c:LANES * (c + 1)]
            return carry

        lax.fori_loop(0, rows // LANES, body, 0)

    for name, args in tokens():
        if name == "own":
            link, m = args[0], int(args[1])
            if link == "P":
                own_copy(link, m).start()
            else:
                @pl.when(end)
                def _():
                    lift_copy(m).start()

                @pl.when(middle)
                def _():
                    own_copy(link, m).start()
        elif name == "comp":
            k = int(args[0])
            if "comp" not in waited:
                need("comp")
                high, low = split(comp[...])
                comp3[:, :rows] = high
                comp3[:, rows:2 * rows] = high
                comp3[:, 2 * rows:] = low
                need("x")
            high, low = split(xv[:, here[k]])
            x_high[:, here[k]] = high
            x_low[:, here[k]] = low
            sent[0, k] = matmul(comp3[...], jnp.concatenate([high, low, high], axis=0))
            far_copy(0, k).start()
        elif name == "L":
            level, k = int(args[0]), int(args[1])
            if "trans" not in waited:
                need("trans")
                for i in range(5):
                    for j in range(2):
                        high, low = split(trans[2 * i + j])
                        at = 3 * rank * j
                        trans6[i, :, at:at + rank] = high
                        trans6[i, :, at + rank:at + 2 * rank] = high
                        trans6[i, :, at + 2 * rank:at + 3 * rank] = low
            far_copy(level, k).wait_recv()
            both = jnp.concatenate([three(sent[level, k]), three(came[level, k])], axis=0)
            coeffs = matmul(trans6[level], both)
            if level < 4:
                sent[level + 1, k] = coeffs
                if level == 3 and k in RELAYED:
                    first_leg(k).start()
                else:
                    far_copy(level + 1, k).start()
            else:
                if "expa" not in waited:
                    need("expa")
                    high, low = split(expa[...].T)
                    expa3[:, :rank] = high
                    expa3[:, rank:2 * rank] = high
                    expa3[:, 2 * rank:] = low
                out[:, here[k]] = out[:, here[k]] + matmul(expa3[...], three(coeffs))
        elif name == "R":
            k = int(args[0])
            first_leg(k).wait_recv()
            second_leg(k).start()
        elif name == "prep":
            prepare(int(args[0]))
        elif name == "ownmm":
            at = slice(cols // 2 * int(args[0]), cols // 2 * (int(args[0]) + 1))
            high = [w_high[OWN, c] for c in range(rows // LANES)]
            low = [w_low[OWN, c] for c in range(rows // LANES)]
            left = jnp.concatenate(high + high + low, axis=1)
            right = jnp.concatenate([x_high[:, at], x_low[:, at], x_high[:, at]], axis=0)
            out[:, at] = matmul(left, right)
        elif name == "Z0":
            m = int(args[0])

            @pl.when(end)
            def _():
                arrived("Z0", "Q", m)
                pass_copy("Z0", "Q", m).start()
        else:
            link, m = args[0], int(args[1])
            arrived(name, link, m)
            if name == "A1":
                pass_copy("A1", link, m).start()
            if name == "A2":
                z_copy(link, m).start()

                @pl.when(end)
                def _():
                    pass_copy("A2", link, m).start()
            if name == "ZR":
                @pl.when(middle)
                def _():
                    pass_copy("ZR", link, m).start()
            if (m + 1) % TOGETHER == 0:
                near_product(name, link, m + 1 - TOGETHER)

    for link in "PQ":
        for m in range(COUNT[link]):
            own_copy(link, m).wait_send()
            z_copy(link, m).wait_send()
            pass_copy("A2", link, m).wait_send()
        for m in range(COUNT[OTHER[link]]):
            pass_copy("A1", link, m).wait_send()

    @pl.when(end)
    def _():
        for m in range(COUNT["Q"]):
            pass_copy("Z0", "Q", m).wait_send()

    for level in range(5):
        for k in range(PARTS):
            far_copy(level, k).wait_send()
    for k in RELAYED:
        second_leg(k).wait_send()


def per_device(charges, near_blocks, neighbours, compress, transfer, expand):
    rows, cols = charges.shape
    rank = compress.shape[2]
    leaves = lax.axis_size("leaf")
    tall, wide = rows // ROUNDS, cols // PARTS
    anywhere = pl.BlockSpec(memory_space=pl.ANY)
    dma = pltpu.SemaphoreType.DMA
    vmem = pltpu.VMEM
    return pl.pallas_call(
        functools.partial(kernel, leaves // XS),
        out_shape=jax.ShapeDtypeStruct((rows, cols), F32),
        in_specs=[pl.BlockSpec(memory_space=pltpu.SMEM)] + [anywhere] * 5,
        out_specs=pl.BlockSpec(memory_space=pltpu.VMEM),
        scratch_shapes=[
            vmem((rows, cols), F32),
            vmem((rows, cols), BF16),
            vmem((rows, cols), BF16),
            vmem((HOLD, tall, cols), F32),
            vmem((5, rows // LANES, rows, LANES), BF16),
            vmem((5, rows // LANES, rows, LANES), BF16),
            vmem((3, rows, rows), F32),
            vmem((rank, rows), F32),
            vmem((rank, 3 * rows), BF16),
            vmem((10, rank, rank), F32),
            vmem((5, rank, 6 * rank), BF16),
            vmem((rank, rows), F32),
            vmem((rows, 3 * rank), BF16),
            vmem((5, PARTS, rank, wide), F32),
            vmem((5, PARTS, rank, wide), F32),
            vmem((len(RELAYED), rank, wide), F32),
            dma((5,)),
            dma((HOLD + ROUNDS,)),
            dma((HOLD,)),
            dma((5, PARTS)),
            dma((5, PARTS)),
            dma((len(RELAYED),)),
            dma((len(RELAYED),)),
        ],
        compiler_params=pltpu.CompilerParams(
            collective_id=0, has_side_effects=True, vmem_limit_bytes=63 << 20),
        name="operator",
    )(
        neighbours,
        charges,
        near_blocks[0],
        compress[0].T,
        transfer[0].reshape(10, rank, rank),
        expand[0].T,
    )


def solution(mesh):
    in_specs = (
        P("leaf", "rhs"),
        P("leaf", None, None, None),
        P("leaf", None),
        P("leaf", None, None),
        P("leaf", None, None, None, None),
        P("leaf", None, None),
    )
    out_specs = P("leaf", "rhs")
    return jax.shard_map(
        per_device, mesh=mesh, in_specs=in_specs, out_specs=out_specs, check_vma=False
    )
```

```python
import functools

import jax
import jax.numpy as jnp
from jax import lax
from jax.experimental import pallas as pl
from jax.experimental.pallas import tpu as pltpu
from jax.sharding import PartitionSpec as P

F32, BF16 = jnp.float32, jnp.bfloat16
XS = 4
PARTS = 4
ROUNDS = 12
TOGETHER = 4
LANES = 128
COUNT = {"P": 4, "Q": 8}
SLOTS = (("A1", "P", 8), ("A1", "Q", 4), ("A2", "P", 4), ("A2", "Q", 8), ("A3", "P", 8),
         ("A3", "Q", 4), ("ZR", "P", 4), ("ZR", "Q", 8), ("Z0", "Q", 8))
BASE, HOLD = {}, 0
for _slot, _link, _count in SLOTS:
    BASE[_slot, _link] = HOLD
    HOLD += _count
OTHER = {"P": "Q", "Q": "P"}
PLUS = {-2: 0, -1: 1, 1: 2, 2: 3}
OWN = 4
RELAYED = (0, 2, 3)

ORDER = (
    "own Q 0", "comp 0", "comp 1", "own Q 1", "prep 2", "L 0 0", "comp 3", "Z0 0", "prep 4",
    "prep 1", "L 0 1", "own P 0", "own Q 2", "Z0 1", "L 1 0", "comp 2", "own Q 3", "Z0 2", "L 2 0",
    "ownmm 0", "L 1 1", "L 0 3", "prep 3", "ownmm 1", "A1 Q 0", "own Q 4", "own P 1", "A1 P 0",
    "A1 P 1", "L 2 1", "L 1 3", "L 3 0", "Z0 3", "prep 0", "A2 P 0", "own Q 5", "A2 Q 0", "L 0 2",
    "own Q 6", "L 2 3", "A1 Q 1", "L 3 1", "own P 2", "A1 P 2", "own P 3", "Z0 4", "ZR P 0",
    "A1 P 3", "A2 P 1", "Z0 5", "A1 Q 2", "L 1 2", "ZR Q 0", "A2 Q 1", "A1 P 4", "Z0 6", "A2 P 2",
    "own Q 7", "A3 Q 0", "A2 Q 2", "L 2 2", "A1 Q 3", "ZR Q 1", "L 3 3", "A1 P 5", "R 0", "ZR P 1",
    "A3 P 0", "A1 P 6", "Z0 7", "A3 P 1", "ZR Q 2", "A2 Q 3", "A2 P 3", "A2 Q 4", "ZR Q 3",
    "A3 P 2", "L 3 2", "A1 P 7", "A3 P 3", "A2 Q 5", "ZR P 2", "R 3", "A3 Q 1", "A3 Q 2", "A2 Q 6",
    "ZR Q 4", "L 4 0", "ZR P 3", "L 4 1", "A3 Q 3", "ZR Q 5", "A2 Q 7", "R 2", "ZR Q 6", "A3 P 4",
    "A3 P 5", "ZR Q 7", "L 4 3", "A3 P 6", "A3 P 7", "L 4 2",
)


def tokens():
    for token in ORDER:
        name, *args = token.split()
        yield name, args


def split(value):
    high = value.astype(BF16)
    return high, (value - high.astype(F32)).astype(BF16)


def three(value):
    high, low = split(value)
    return jnp.concatenate([high, low, high], axis=0)


def matmul(left, right):
    return jnp.dot(left, right, preferred_element_type=F32)


def kernel(zs, nb, x_hbm, near_hbm, compress_hbm, transfer_hbm, expand_hbm, out,
           xv, x_high, x_low, got, w_high, w_low, near, comp, comp3, trans, trans6,
           expa, expa3, sent, came, mid, load_sem, near_send, near_recv, far_send, far_recv,
           mid_send, mid_recv):
    rows, cols = out.shape
    tall, wide = rows // ROUNDS, cols // PARTS
    rank = comp3.shape[0]
    leaf, r = lax.axis_index("leaf"), lax.axis_index("rhs")
    x, z = leaf % XS, leaf // XS
    odd = x % 2
    step = {"P": 1 - 2 * odd, "Q": 2 * odd - 1}
    end = jnp.logical_or(x == 0, x == XS - 1)
    middle = jnp.logical_not(end)

    def chip(dx, dz):
        return ((z + dz + zs) % zs) * XS + (x + dx + XS) % XS, r

    def partner(level):
        bit = (leaf // 2**level) % 2
        return leaf + (1 - 2 * bit) * 2**level, r

    def load(i, src, dst):
        return pltpu.make_async_copy(src, dst, load_sem.at[i])

    loads = {
        "comp": load(0, compress_hbm, comp),
        "x": load(1, x_hbm, xv),
        "trans": load(2, transfer_hbm, trans),
        "near": load(3, near_hbm, near),
        "expa": load(4, expand_hbm, expa),
    }
    for item in loads.values():
        item.start()

    barrier = pltpu.get_barrier_semaphore()
    greeted = [chip(1, 0), chip(-1, 0), partner(1), chip(0, 1), chip(0, -1), chip(0, 2),
               chip(0, -2), partner(4)]
    for device in greeted:
        pl.semaphore_signal(barrier, inc=1, device_id=device, device_id_type=pl.DeviceIdType.MESH)
    pl.semaphore_wait(barrier, len(greeted))

    def remote(src, dst, send, recv, device):
        return pltpu.make_async_remote_copy(
            src_ref=src, dst_ref=dst, send_sem=send, recv_sem=recv,
            device_id=device, device_id_type=pl.DeviceIdType.MESH)

    def near_copy(send, src, slot, link, m, device):
        at = BASE[slot, link] + m
        return remote(src, got.at[at], near_send.at[send], near_recv.at[at], device)

    def own_rows(link, m):
        first = jnp.where(step[link] == 1, 0, ROUNDS - COUNT[link])
        return x_hbm.at[pl.ds(pl.multiple_of(tall * (first + m), tall), tall)]

    def own_copy(link, m):
        return near_copy(HOLD + m + COUNT["Q"] * (link == "P"), own_rows(link, m), "A1", OTHER[link], m,
                         chip(step[link], 0))

    def lift_copy(m):
        return near_copy(HOLD + m, own_rows("Q", m), "Z0", "Q", m, chip(0, step["Q"]))

    def pass_copy(slot, link, m):
        source = BASE[slot, link] + m
        to = {"Z0": "A1", "A1": "A2", "A2": "A3", "ZR": "A3"}[slot]
        send = BASE["A3", OTHER[link]] + m if to == "A3" else source
        return near_copy(send, got.at[source], to, OTHER[link], m, chip(step[link], 0))

    def z_copy(link, m):
        h = jnp.where(step[link] == 1, 0, 1)
        wraps = x == (XS - 1) * h
        dz = jnp.where(wraps, 1, -1) * step[link]
        source = BASE["A2", link] + m
        return near_copy(source, got.at[source], "ZR", link, m, chip(0, dz))

    def arrived(slot, link, m):
        at = BASE[slot, link] + m
        remote(got.at[at], got.at[at], near_send.at[at], near_recv.at[at], chip(1, 0)).wait_recv()

    def weight_of(slot, link):
        h = jnp.where(step[link] == 1, 0, 1)
        if slot == "A1":
            return 1 + h
        if slot == "A3":
            return 2 - h
        wraps = x == (XS - 1) * h
        ahead, behind = 3 - 3 * h, 3 * h
        if slot == "A2":
            return jnp.where(wraps, ahead, behind)
        return jnp.where(wraps, behind, ahead)

    def near_product(slot, link, m):
        which = weight_of(slot, link)
        count = dict(((a, b), c) for a, b, c in SLOTS)[slot, link]
        first = (jnp.where(step[link] == 1, 0, ROUNDS - count) + m) * tall // LANES
        at = BASE[slot, link] + m
        pieces = TOGETHER * tall // LANES
        high = [w_high[which, first + i] for i in range(pieces)]
        low = [w_low[which, first + i] for i in range(pieces)]
        left = jnp.concatenate(high + high + low, axis=1)
        for to in (slice(0, cols // 2), slice(cols // 2, cols)):
            value = jnp.concatenate([got[at + i, :, to] for i in range(TOGETHER)], axis=0)
            out[:, to] = out[:, to] + matmul(left, three(value))

    def far_copy(level, k):
        return remote(sent.at[level, k], came.at[level, k], far_send.at[level, k],
                      far_recv.at[level, k], partner(level))

    two_on = chip(0, 4 * odd - 2)

    def first_leg(k):
        i = RELAYED.index(k)
        return remote(sent.at[4, k], mid.at[i], far_send.at[4, k], mid_recv.at[i], two_on)

    def second_leg(k):
        i = RELAYED.index(k)
        return remote(mid.at[i], came.at[4, k], mid_send.at[i], far_recv.at[4, k], two_on)

    here = [pl.ds(wide * k, wide) for k in range(PARTS)]
    waited = set()

    def need(name):
        if name not in waited:
            waited.add(name)
            loads[name].wait()

    def prepare(which):
        need("near")
        if which == OWN:
            scales = None
        else:
            offset = {v: k for k, v in PLUS.items()}[which]
            count = zs * XS
            scales = [
                jnp.where((nb[0, j] - leaf - offset + 2 * count) % count == 0, 1.0, 0.0).astype(F32)
                for j in range(2)
            ]

        def body(i, carry):
            at = pl.ds(pl.multiple_of(i * LANES, LANES), LANES)
            if scales is None:
                value = near[0, at, :]
            else:
                value = scales[0] * near[1, at, :] + scales[1] * near[2, at, :]
            high, low = split(value)
            for c in range(rows // LANES):
                w_high[which, c, at, :] = high[:, LANES * c:LANES * (c + 1)]
                w_low[which, c, at, :] = low[:, LANES * c:LANES * (c + 1)]
            return carry

        lax.fori_loop(0, rows // LANES, body, 0)

    for name, args in tokens():
        if name == "own":
            link, m = args[0], int(args[1])
            if link == "P":
                own_copy(link, m).start()
            else:
                @pl.when(end)
                def _():
                    lift_copy(m).start()

                @pl.when(middle)
                def _():
                    own_copy(link, m).start()
        elif name == "comp":
            k = int(args[0])
            if "comp" not in waited:
                need("comp")
                high, low = split(comp[...])
                comp3[:, :rows] = high
                comp3[:, rows:2 * rows] = high
                comp3[:, 2 * rows:] = low
                need("x")
            high, low = split(xv[:, here[k]])
            x_high[:, here[k]] = high
            x_low[:, here[k]] = low
            sent[0, k] = matmul(comp3[...], jnp.concatenate([high, low, high], axis=0))
            far_copy(0, k).start()
        elif name == "L":
            level, k = int(args[0]), int(args[1])
            if "trans" not in waited:
                need("trans")
                for i in range(5):
                    for j in range(2):
                        high, low = split(trans[2 * i + j])
                        at = 3 * rank * j
                        trans6[i, :, at:at + rank] = high
                        trans6[i, :, at + rank:at + 2 * rank] = high
                        trans6[i, :, at + 2 * rank:at + 3 * rank] = low
            far_copy(level, k).wait_recv()
            both = jnp.concatenate([three(sent[level, k]), three(came[level, k])], axis=0)
            coeffs = matmul(trans6[level], both)
            if level < 4:
                sent[level + 1, k] = coeffs
                if level == 3 and k in RELAYED:
                    first_leg(k).start()
                else:
                    far_copy(level + 1, k).start()
            else:
                if "expa" not in waited:
                    need("expa")
                    high, low = split(expa[...].T)
                    expa3[:, :rank] = high
                    expa3[:, rank:2 * rank] = high
                    expa3[:, 2 * rank:] = low
                out[:, here[k]] = out[:, here[k]] + matmul(expa3[...], three(coeffs))
        elif name == "R":
            k = int(args[0])
            first_leg(k).wait_recv()
            second_leg(k).start()
        elif name == "prep":
            prepare(int(args[0]))
        elif name == "ownmm":
            at = slice(cols // 2 * int(args[0]), cols // 2 * (int(args[0]) + 1))
            high = [w_high[OWN, c] for c in range(rows // LANES)]
            low = [w_low[OWN, c] for c in range(rows // LANES)]
            left = jnp.concatenate(high + high + low, axis=1)
            right = jnp.concatenate([x_high[:, at], x_low[:, at], x_high[:, at]], axis=0)
            out[:, at] = matmul(left, right)
        elif name == "Z0":
            m = int(args[0])

            @pl.when(end)
            def _():
                arrived("Z0", "Q", m)
                pass_copy("Z0", "Q", m).start()
        else:
            link, m = args[0], int(args[1])
            arrived(name, link, m)
            if name == "A1":
                pass_copy("A1", link, m).start()
            if name == "A2":
                z_copy(link, m).start()

                @pl.when(end)
                def _():
                    pass_copy("A2", link, m).start()
            if name == "ZR":
                @pl.when(middle)
                def _():
                    pass_copy("ZR", link, m).start()
            if (m + 1) % TOGETHER == 0:
                near_product(name, link, m + 1 - TOGETHER)

    for link in "PQ":
        for m in range(COUNT[link]):
            own_copy(link, m).wait_send()
            z_copy(link, m).wait_send()
            pass_copy("A2", link, m).wait_send()
        for m in range(COUNT[OTHER[link]]):
            pass_copy("A1", link, m).wait_send()

    @pl.when(end)
    def _():
        for m in range(COUNT["Q"]):
            pass_copy("Z0", "Q", m).wait_send()

    for level in range(5):
        for k in range(PARTS):
            far_copy(level, k).wait_send()
    for k in RELAYED:
        second_leg(k).wait_send()


def per_device(charges, near_blocks, neighbours, compress, transfer, expand):
    rows, cols = charges.shape
    rank = compress.shape[2]
    leaves = lax.axis_size("leaf")
    tall, wide = rows // ROUNDS, cols // PARTS
    anywhere = pl.BlockSpec(memory_space=pl.ANY)
    dma = pltpu.SemaphoreType.DMA
    vmem = pltpu.VMEM
    return pl.pallas_call(
        functools.partial(kernel, leaves // XS),
        out_shape=jax.ShapeDtypeStruct((rows, cols), F32),
        in_specs=[pl.BlockSpec(memory_space=pltpu.SMEM)] + [anywhere] * 5,
        out_specs=pl.BlockSpec(memory_space=pltpu.VMEM),
        scratch_shapes=[
            vmem((rows, cols), F32),
            vmem((rows, cols), BF16),
            vmem((rows, cols), BF16),
            vmem((HOLD, tall, cols), F32),
            vmem((5, rows // LANES, rows, LANES), BF16),
            vmem((5, rows // LANES, rows, LANES), BF16),
            vmem((3, rows, rows), F32),
            vmem((rank, rows), F32),
            vmem((rank, 3 * rows), BF16),
            vmem((10, rank, rank), F32),
            vmem((5, rank, 6 * rank), BF16),
            vmem((rank, rows), F32),
            vmem((rows, 3 * rank), BF16),
            vmem((5, PARTS, rank, wide), F32),
            vmem((5, PARTS, rank, wide), F32),
            vmem((len(RELAYED), rank, wide), F32),
            dma((5,)),
            dma((HOLD + ROUNDS,)),
            dma((HOLD,)),
            dma((5, PARTS)),
            dma((5, PARTS)),
            dma((len(RELAYED),)),
            dma((len(RELAYED),)),
        ],
        compiler_params=pltpu.CompilerParams(
            collective_id=0, has_side_effects=True, vmem_limit_bytes=63 << 20),
        name="operator",
    )(
        neighbours,
        charges,
        near_blocks[0],
        compress[0].T,
        transfer[0].reshape(10, rank, rank),
        expand[0].T,
    )


def solution(mesh):
    in_specs = (
        P("leaf", "rhs"),
        P("leaf", None, None, None),
        P("leaf", None),
        P("leaf", None, None),
        P("leaf", None, None, None, None),
        P("leaf", None, None),
    )
    out_specs = P("leaf", "rhs")
    return jax.shard_map(
        per_device, mesh=mesh, in_specs=in_specs, out_specs=out_specs, check_vma=False
    )
```

```python
import functools

import jax
import jax.numpy as jnp
from jax import lax
from jax.experimental import pallas as pl
from jax.experimental.pallas import tpu as pltpu
from jax.sharding import PartitionSpec as P

F32, BF16 = jnp.float32, jnp.bfloat16
XS = 4
PARTS = 4
ROUNDS = 12
TOGETHER = 4
LANES = 128
COUNT = {"P": 4, "Q": 8}
SLOTS = (("A1", "P", 8), ("A1", "Q", 4), ("A2", "P", 4), ("A2", "Q", 8), ("A3", "P", 8),
         ("A3", "Q", 4), ("ZR", "P", 4), ("ZR", "Q", 8), ("Z0", "Q", 8))
BASE, HOLD = {}, 0
for _slot, _link, _count in SLOTS:
    BASE[_slot, _link] = HOLD
    HOLD += _count
OTHER = {"P": "Q", "Q": "P"}
SPARE = {"A1": 0, "A2": 1, "A3": 2, "ZR": 3}
SHARED = 2
PLUS = {-2: 0, -1: 1, 1: 2, 2: 3}
OWN = 4
RELAYED = (0, 3)

ORDER = (
    "own Q 0", "comp 0", "own Q 1", "Z0 0", "comp 1", "L 0 0", "prep 2", "L 0 1", "Z0 1", "comp 3",
    "own Q 2", "L 1 0", "comp 2", "prep 4", "own Q 3", "L 1 1", "own Q 4", "prep 1", "Z0 2",
    "L 2 0", "L 0 3", "own P 0", "ownmm 1", "ownmm 0", "L 2 1", "prep 0", "A1 P 0", "A1 Q 0",
    "prep 3", "own P 1", "own P 2", "A2 Q 0", "A1 P 1", "Z0 3", "L 1 3", "own P 3", "A2 P 0",
    "own Q 5", "Z0 4", "own P 4", "ZR Q 0", "L 2 3", "A3 P 0", "L 0 2", "A1 Q 1", "A1 Q 2",
    "L 3 1", "L 3 0", "A2 Q 1", "A2 P 1", "Z0 5", "ZR P 0", "A1 P 2", "A1 P 3", "L 1 2", "A2 P 2",
    "ZR Q 1", "A1 Q 3", "A3 P 1", "A2 Q 2", "own Q 6", "L 3 3", "ZR P 1", "A3 Q 0", "A1 P 4",
    "A1 P 5", "own Q 7", "ZR P 2", "L 2 2", "Z0 6", "A2 Q 3", "R 0", "ZR Q 2", "R 3", "A1 P 6",
    "A2 Q 4", "Z0 7", "ZR Q 3", "A2 P 3", "L 4 1", "A1 Q 4", "A2 Q 5", "A3 P 2", "A3 P 3",
    "ZR Q 4", "A1 P 7", "A2 Q 6", "ZR Q 5", "A2 Q 7", "ZR Q 6", "A3 Q 1", "A2 P 4", "ZR P 3",
    "L 3 2", "A3 P 4", "ZR Q 7", "A3 Q 2", "ZR P 4", "A3 P 5", "L 4 3", "L 4 0", "A3 P 6",
    "A3 Q 3", "A3 Q 4", "A3 P 7", "L 4 2",
)


def tokens():
    for token in ORDER:
        name, *args = token.split()
        yield name, args


def split(value):
    high = value.astype(BF16)
    return high, (value - high.astype(F32)).astype(BF16)


def three(value):
    high, low = split(value)
    return jnp.concatenate([high, low, high], axis=0)


def matmul(left, right):
    return jnp.dot(left, right, preferred_element_type=F32)


def kernel(zs, nb, x_hbm, near_hbm, compress_hbm, transfer_hbm, expand_hbm, out,
           xv, x_high, x_low, got, w_high, w_low, near, comp, comp3, trans, trans6,
           expa, expa3, sent, came, mid, spare, load_sem, near_send, near_recv, far_send, far_recv,
           mid_send, mid_recv, spare_send, spare_recv):
    rows, cols = out.shape
    tall, wide = rows // ROUNDS, cols // PARTS
    rank = comp3.shape[0]
    leaf, r = lax.axis_index("leaf"), lax.axis_index("rhs")
    x, z = leaf % XS, leaf // XS
    odd = x % 2
    step = {"P": 1 - 2 * odd, "Q": 2 * odd - 1}
    end = jnp.logical_or(x == 0, x == XS - 1)
    middle = jnp.logical_not(end)

    def chip(dx, dz):
        return ((z + dz + zs) % zs) * XS + (x + dx + XS) % XS, r

    def partner(level):
        bit = (leaf // 2**level) % 2
        return leaf + (1 - 2 * bit) * 2**level, r

    def load(i, src, dst):
        return pltpu.make_async_copy(src, dst, load_sem.at[i])

    loads = {
        "comp": load(0, compress_hbm, comp),
        "x": load(1, x_hbm, xv),
        "trans": load(2, transfer_hbm, trans),
        "near": load(3, near_hbm, near),
        "expa": load(4, expand_hbm, expa),
    }
    for item in loads.values():
        item.start()

    barrier = pltpu.get_barrier_semaphore()
    greeted = [chip(1, 0), chip(-1, 0), partner(1), chip(0, 1), chip(0, -1), chip(0, 2),
               chip(0, -2), partner(4)]
    for device in greeted:
        pl.semaphore_signal(barrier, inc=1, device_id=device, device_id_type=pl.DeviceIdType.MESH)
    pl.semaphore_wait(barrier, len(greeted))

    def remote(src, dst, send, recv, device):
        return pltpu.make_async_remote_copy(
            src_ref=src, dst_ref=dst, send_sem=send, recv_sem=recv,
            device_id=device, device_id_type=pl.DeviceIdType.MESH)

    counts = {(a, b): c for a, b, c in SLOTS}

    def near_copy(send, src, slot, link, m, device):
        at = BASE[slot, link] + m
        dst = got.at[at]
        if counts[slot, link] == COUNT["Q"] and m < SHARED:
            most = pl.ds(wide, cols - wide)
            src, dst = src.at[:, most], dst.at[:, most]
        return remote(src, dst, near_send.at[send], near_recv.at[at], device)

    def spare_copy(send, src, slot, device):
        at = SPARE[slot]
        return remote(src, spare.at[at], spare_send.at[send], spare_recv.at[at], device)

    def spare_own():
        first = tall * jnp.where(step["Q"] == 1, 0, ROUNDS - COUNT["Q"])
        src = x_hbm.at[pl.ds(pl.multiple_of(first, tall), SHARED * tall), pl.ds(0, wide)]
        return spare_copy(0, src, "A1", chip(step["P"], 0))

    def spare_pass(slot, link):
        to, send = ("A2", 1) if slot == "A1" else ("A3", 2)
        return spare_copy(send, spare.at[SPARE[slot]], to, chip(step[link], 0))

    def spare_z():
        return spare_copy(3, spare.at[SPARE["A2"]], "ZR", chip(0, z_step("P")))

    def own_rows(link, m):
        first = jnp.where(step[link] == 1, 0, ROUNDS - COUNT[link])
        return x_hbm.at[pl.ds(pl.multiple_of(tall * (first + m), tall), tall)]

    def own_copy(link, m):
        return near_copy(HOLD + m + COUNT["Q"] * (link == "P"), own_rows(link, m), "A1", OTHER[link], m,
                         chip(step[link], 0))

    def lift_copy(m):
        return near_copy(HOLD + m, own_rows("Q", m), "Z0", "Q", m, chip(0, step["Q"]))

    def pass_copy(slot, link, m):
        source = BASE[slot, link] + m
        to = {"Z0": "A1", "A1": "A2", "A2": "A3", "ZR": "A3"}[slot]
        send = BASE["A3", OTHER[link]] + m if to == "A3" else source
        return near_copy(send, got.at[source], to, OTHER[link], m, chip(step[link], 0))

    def z_step(link):
        h = jnp.where(step[link] == 1, 0, 1)
        wraps = x == (XS - 1) * h
        return jnp.where(wraps, 1, -1) * step[link]

    def z_copy(link, m):
        source = BASE["A2", link] + m
        return near_copy(source, got.at[source], "ZR", link, m, chip(0, z_step(link)))

    def arrived(slot, link, m):
        at = BASE[slot, link] + m
        near_copy(at, got.at[at], slot, link, m, chip(1, 0)).wait_recv()

    def weight_of(slot, link):
        h = jnp.where(step[link] == 1, 0, 1)
        if slot == "A1":
            return 1 + h
        if slot == "A3":
            return 2 - h
        wraps = x == (XS - 1) * h
        ahead, behind = 3 - 3 * h, 3 * h
        if slot == "A2":
            return jnp.where(wraps, ahead, behind)
        return jnp.where(wraps, behind, ahead)

    def near_product(slot, link, m):
        which = weight_of(slot, link)
        count = counts[slot, link]
        first = (jnp.where(step[link] == 1, 0, ROUNDS - count) + m) * tall // LANES
        at = BASE[slot, link] + m

        def add(skip, to):
            pieces = range(skip * tall // LANES, TOGETHER * tall // LANES)
            high = [w_high[which, first + i] for i in pieces]
            low = [w_low[which, first + i] for i in pieces]
            left = jnp.concatenate(high + high + low, axis=1)
            value = jnp.concatenate([got[at + i, :, to] for i in range(skip, TOGETHER)], axis=0)
            out[:, to] = out[:, to] + matmul(left, three(value))

        if count == COUNT["Q"] and m == 0:
            add(SHARED, slice(0, wide))
            add(0, slice(wide, cols // 2))
        else:
            add(0, slice(0, cols // 2))
        add(0, slice(cols // 2, cols))

    def spare_product(slot, link):
        which = weight_of(slot, link)
        piece = jnp.where(step[link] == 1, (ROUNDS - COUNT["Q"]) * tall // LANES, 0)
        high, low = w_high[which, piece], w_low[which, piece]
        left = jnp.concatenate([high, high, low], axis=1)
        out[:, :wide] = out[:, :wide] + matmul(left, three(spare[SPARE[slot]]))

    def far_copy(level, k):
        return remote(sent.at[level, k], came.at[level, k], far_send.at[level, k],
                      far_recv.at[level, k], partner(level))

    two_on = chip(0, 4 * odd - 2)

    def first_leg(k):
        i = RELAYED.index(k)
        return remote(sent.at[4, k], mid.at[i], far_send.at[4, k], mid_recv.at[i], two_on)

    def second_leg(k):
        i = RELAYED.index(k)
        return remote(mid.at[i], came.at[4, k], mid_send.at[i], far_recv.at[4, k], two_on)

    here = [pl.ds(wide * k, wide) for k in range(PARTS)]
    waited = set()

    def need(name):
        if name not in waited:
            waited.add(name)
            loads[name].wait()

    def prepare(which):
        need("near")
        if which == OWN:
            scales = None
        else:
            offset = {v: k for k, v in PLUS.items()}[which]
            count = zs * XS
            scales = [
                jnp.where((nb[0, j] - leaf - offset + 2 * count) % count == 0, 1.0, 0.0).astype(F32)
                for j in range(2)
            ]

        def body(i, carry):
            at = pl.ds(pl.multiple_of(i * LANES, LANES), LANES)
            if scales is None:
                value = near[0, at, :]
            else:
                value = scales[0] * near[1, at, :] + scales[1] * near[2, at, :]
            high, low = split(value)
            for c in range(rows // LANES):
                w_high[which, c, at, :] = high[:, LANES * c:LANES * (c + 1)]
                w_low[which, c, at, :] = low[:, LANES * c:LANES * (c + 1)]
            return carry

        lax.fori_loop(0, rows // LANES, body, 0)

    for name, args in tokens():
        if name == "own":
            link, m = args[0], int(args[1])
            if link == "P" and m == COUNT["P"]:
                spare_own().start()
            elif link == "P":
                own_copy(link, m).start()
            else:
                @pl.when(end)
                def _():
                    lift_copy(m).start()

                @pl.when(middle)
                def _():
                    own_copy(link, m).start()
        elif name == "comp":
            k = int(args[0])
            if "comp" not in waited:
                need("comp")
                high, low = split(comp[...])
                comp3[:, :rows] = high
                comp3[:, rows:2 * rows] = high
                comp3[:, 2 * rows:] = low
                need("x")
            high, low = split(xv[:, here[k]])
            x_high[:, here[k]] = high
            x_low[:, here[k]] = low
            sent[0, k] = matmul(comp3[...], jnp.concatenate([high, low, high], axis=0))
            far_copy(0, k).start()
        elif name == "L":
            level, k = int(args[0]), int(args[1])
            if "trans" not in waited:
                need("trans")
                for i in range(5):
                    for j in range(2):
                        high, low = split(trans[2 * i + j])
                        at = 3 * rank * j
                        trans6[i, :, at:at + rank] = high
                        trans6[i, :, at + rank:at + 2 * rank] = high
                        trans6[i, :, at + 2 * rank:at + 3 * rank] = low
            far_copy(level, k).wait_recv()
            both = jnp.concatenate([three(sent[level, k]), three(came[level, k])], axis=0)
            coeffs = matmul(trans6[level], both)
            if level < 4:
                sent[level + 1, k] = coeffs
                if level == 3 and k in RELAYED:
                    first_leg(k).start()
                else:
                    far_copy(level + 1, k).start()
            else:
                if "expa" not in waited:
                    need("expa")
                    high, low = split(expa[...].T)
                    expa3[:, :rank] = high
                    expa3[:, rank:2 * rank] = high
                    expa3[:, 2 * rank:] = low
                out[:, here[k]] = out[:, here[k]] + matmul(expa3[...], three(coeffs))
        elif name == "R":
            k = int(args[0])
            first_leg(k).wait_recv()
            second_leg(k).start()
        elif name == "prep":
            prepare(int(args[0]))
        elif name == "ownmm":
            at = slice(cols // 2 * int(args[0]), cols // 2 * (int(args[0]) + 1))
            high = [w_high[OWN, c] for c in range(rows // LANES)]
            low = [w_low[OWN, c] for c in range(rows // LANES)]
            left = jnp.concatenate(high + high + low, axis=1)
            right = jnp.concatenate([x_high[:, at], x_low[:, at], x_high[:, at]], axis=0)
            out[:, at] = matmul(left, right)
        elif name == "Z0":
            m = int(args[0])

            @pl.when(end)
            def _():
                arrived("Z0", "Q", m)
                pass_copy("Z0", "Q", m).start()
        elif int(args[1]) == counts[name, args[0]]:
            link = args[0]
            spare_copy(0, spare.at[SPARE[name]], name, chip(1, 0)).wait_recv()
            if name == "A1":
                spare_pass("A1", link).start()
            if name == "A2":
                spare_z().start()

                @pl.when(end)
                def _():
                    spare_pass("A2", link).start()
            if name == "ZR":
                @pl.when(middle)
                def _():
                    spare_pass("ZR", link).start()
            spare_product(name, link)
        else:
            link, m = args[0], int(args[1])
            arrived(name, link, m)
            if name == "A1":
                pass_copy("A1", link, m).start()
            if name == "A2":
                z_copy(link, m).start()

                @pl.when(end)
                def _():
                    pass_copy("A2", link, m).start()
            if name == "ZR":
                @pl.when(middle)
                def _():
                    pass_copy("ZR", link, m).start()
            if (m + 1) % TOGETHER == 0:
                near_product(name, link, m + 1 - TOGETHER)

    spare_own().wait_send()
    spare_pass("A1", "Q").wait_send()
    spare_pass("A2", "P").wait_send()
    spare_z().wait_send()
    for link in "PQ":
        for m in range(COUNT[link]):
            own_copy(link, m).wait_send()
            z_copy(link, m).wait_send()
            pass_copy("A2", link, m).wait_send()
        for m in range(COUNT[OTHER[link]]):
            pass_copy("A1", link, m).wait_send()

    @pl.when(end)
    def _():
        for m in range(COUNT["Q"]):
            pass_copy("Z0", "Q", m).wait_send()

    for level in range(5):
        for k in range(PARTS):
            far_copy(level, k).wait_send()
    for k in RELAYED:
        second_leg(k).wait_send()


def per_device(charges, near_blocks, neighbours, compress, transfer, expand):
    rows, cols = charges.shape
    rank = compress.shape[2]
    leaves = lax.axis_size("leaf")
    tall, wide = rows // ROUNDS, cols // PARTS
    anywhere = pl.BlockSpec(memory_space=pl.ANY)
    dma = pltpu.SemaphoreType.DMA
    vmem = pltpu.VMEM
    return pl.pallas_call(
        functools.partial(kernel, leaves // XS),
        out_shape=jax.ShapeDtypeStruct((rows, cols), F32),
        in_specs=[pl.BlockSpec(memory_space=pltpu.SMEM)] + [anywhere] * 5,
        out_specs=pl.BlockSpec(memory_space=pltpu.VMEM),
        scratch_shapes=[
            vmem((rows, cols), F32),
            vmem((rows, cols), BF16),
            vmem((rows, cols), BF16),
            vmem((HOLD, tall, cols), F32),
            vmem((5, rows // LANES, rows, LANES), BF16),
            vmem((5, rows // LANES, rows, LANES), BF16),
            vmem((3, rows, rows), F32),
            vmem((rank, rows), F32),
            vmem((rank, 3 * rows), BF16),
            vmem((10, rank, rank), F32),
            vmem((5, rank, 6 * rank), BF16),
            vmem((rank, rows), F32),
            vmem((rows, 3 * rank), BF16),
            vmem((5, PARTS, rank, wide), F32),
            vmem((5, PARTS, rank, wide), F32),
            vmem((len(RELAYED), rank, wide), F32),
            vmem((len(SPARE), SHARED * tall, wide), F32),
            dma((5,)),
            dma((HOLD + ROUNDS,)),
            dma((HOLD,)),
            dma((5, PARTS)),
            dma((5, PARTS)),
            dma((len(RELAYED),)),
            dma((len(RELAYED),)),
            dma((len(SPARE),)),
            dma((len(SPARE),)),
        ],
        compiler_params=pltpu.CompilerParams(
            collective_id=0, has_side_effects=True, vmem_limit_bytes=63 << 20),
        name="operator",
    )(
        neighbours,
        charges,
        near_blocks[0],
        compress[0].T,
        transfer[0].reshape(10, rank, rank),
        expand[0].T,
    )


def solution(mesh):
    in_specs = (
        P("leaf", "rhs"),
        P("leaf", None, None, None),
        P("leaf", None),
        P("leaf", None, None),
        P("leaf", None, None, None, None),
        P("leaf", None, None),
    )
    out_specs = P("leaf", "rhs")
    return jax.shard_map(
        per_device, mesh=mesh, in_specs=in_specs, out_specs=out_specs, check_vma=False
    )
```
